128 devices in a mesh: rcpt: 8 (over x, y_hi), space: 16 (over z, y_lo, core).
Axes of the slice: x: 4, y: 4 (y_hi: 2, y_lo: 2; y = y_hi * 2 + y_lo), z: 4, core: 2. Of those that a mesh axis runs over, the one named last changes fastest.
Arguments:
- adjoint_end: float32 [64, 4, 512, 1024], P('rcpt', None, 'space'), may hold values from -6 to 6
- currents: bfloat16 [8, 2, 4, 512, 1024], P('rcpt', None, None, 'space'), may hold values from -0.29882812 to 0.29882812
- plan: int32 [4], replicated, may hold values from 0 to 7, as said below
- water_mask: int32 [512, 1024], P('space'), may hold values 0 or 1
- mixing: float32 [3, 512, 1024], P(None, 'space'), may hold values from 0.02 to 0.2
- decay: float32 [64], P('rcpt'), may hold values from 0.02 to 0.5
- obs_weight: float32 [4, 64], P(None, 'rcpt'), may hold values from 0.3 to 3
- release_cells: int32 [16, 128, 128], P('space'), may hold values from 0 to 32767
- profiles: float32 [16, 128, 512, 128], P(None, ('rcpt', 'space')), may hold values from -0.25 to 0.25
Outputs:
- adjoint_start: float32 [64, 4, 512, 1024], P('rcpt', None, 'space')
- sensitivity: float32 [16, 128, 64, 128], P(None, ('rcpt', 'space'))
The draws below stay inside these ranges and needn't reach their ends.
Inputs may be any that keep to these rules, and one draw needn't show every extreme that they name: 4 distinct store slots; hour h's currents are currents[plan[h]], held by rcpt index plan[h].
All inputs are finite; a program needn't handle non-finite values. No bound on the sum of `water_mask` on one device may be relied on, other than what follows from the above.
Results may differ from the reference program's by a relative error of at most 0.0003.
Values may be sent and summed in bfloat16 or wider, within the bound.
No kernel may reach another device: no remote copies, remote signals or barrier semaphores. Data moves between devices by JAX's collectives and lax.ppermute only.
A program may use at most 256 MiB of HBM per device.

```python
import math
import jax
import jax.numpy as jnp
from jax import lax

CX = 32
NY = 1024
LEVELS = 4
HOURS = 4
CB = 128
P_SIZE = 128
RECEPTORS = 64
NS = 16
NX = 512
STORE = 8
BLK_STRIP = 128


def draw_plan(key, part):
    return jax.random.permutation(key, STORE)[:HOURS].astype(jnp.int32)


def touch_ends(array, own_key, least, largest):
    longest = array.shape.index(max(array.shape))
    spots = []
    for shift in (0, 1):
        where = [jax.random.randint(jax.random.fold_in(own_key, axis), (), 0, length) for axis, length in enumerate(array.shape)]
        where[longest] = (where[longest] + shift) % array.shape[longest]
        spots.append(tuple(where))
    return array.at[spots[0]].set(least).at[spots[1]].set(largest)


def block_levels(own_key, extent, pieces, least, largest):
    gain = 1.0
    for position, parts in pieces:
        steps = jax.random.uniform(jax.random.fold_in(jax.random.fold_in(own_key, 6), position), (parts,), jnp.float32, least / len(pieces), largest / len(pieces))
        gain = gain * jnp.repeat(jnp.exp(steps), extent[position] // parts).reshape((-1,) + (1,) * (len(extent) - 1 - position))
    return gain


def scatter_about(key, extent, width, reach, cuts=(), kind=jnp.bfloat16):
    array = width * jax.random.normal(key, extent, jnp.float32)
    if cuts:
        array = array * block_levels(key, extent, cuts, -0.22, 0.18)
    return jnp.clip(array, -reach, reach).astype(kind)


def setup_inputs(seed: int = 0) -> dict:
    key_list = jax.random.split(jax.random.key(seed), 10)
    adjoint_end = scatter_about(key_list[0], (RECEPTORS, LEVELS, NX, NY), 1.0, 6.0, ((0, 8), (2, 16)), jnp.float32)
    currents = jnp.clip(jax.random.uniform(key_list[1], (STORE, 2, LEVELS, NX, NY), jnp.float32, -0.29882812, 0.29882812) * block_levels(key_list[1], (STORE, 2, LEVELS, NX, NY), ((0, 8), (3, 16)), -0.4, 0.0), -0.29882812, 0.29882812).astype(jnp.bfloat16)
    plan = draw_plan(jax.random.fold_in(key_list[9], 71), 0)
    water_mask = touch_ends((jax.random.randint(key_list[3], (NX, NY), 0, 8) < 7).astype(jnp.int32), jax.random.fold_in(key_list[3], 1), 0, 1)
    mixing = jnp.clip(0.02 + 0.18 * jax.random.uniform(key_list[4], (LEVELS - 1, NX, NY), jnp.float32) ** block_levels(key_list[4], (LEVELS - 1, NX, NY), ((1, 16),), -0.2, 0.2), 0.02, 0.2)
    decay = jnp.clip(jnp.exp(math.log(0.5) - 3.218876 * jax.random.uniform(key_list[5], (RECEPTORS,), jnp.float32) ** block_levels(key_list[5], (RECEPTORS,), ((0, 8),), -0.2, 0.2)), 0.02, 0.5)
    obs_weight = jnp.clip(jnp.exp(math.log(3.0) - 2.3025851 * jax.random.uniform(key_list[6], (HOURS, RECEPTORS), jnp.float32) ** block_levels(key_list[6], (HOURS, RECEPTORS), ((1, 8),), -0.2, 0.2)), 0.3, 3.0)
    release_cells = touch_ends(jax.random.randint(key_list[7], (NS, BLK_STRIP, CB), 0, CX * NY), jax.random.fold_in(key_list[7], 1), 0, (CX * NY) - 1).astype(jnp.int32)
    profiles = scatter_about(key_list[8], (NS, BLK_STRIP, LEVELS * CB, P_SIZE), (LEVELS * CB) ** -0.5, 0.25, ((1, 128),), jnp.float32)
    return dict(adjoint_end=adjoint_end, currents=currents, plan=plan, water_mask=water_mask, mixing=mixing, decay=decay, obs_weight=obs_weight, release_cells=release_cells, profiles=profiles)


diffusion_number = 0.08


def transport(padded, water, current, mixing):
    center = padded[:, :, 1:-1, 1:-1]
    along = current[0].astype(jnp.float32)
    across = current[1].astype(jnp.float32)
    inner = water[1:-1, 1:-1]
    weight_down = (jax.nn.relu(along) + diffusion_number) * water[2:, 1:-1]
    weight_up = (jax.nn.relu(-along) + diffusion_number) * water[:-2, 1:-1]
    weight_right = (jax.nn.relu(across) + diffusion_number) * water[1:-1, 2:]
    weight_left = (jax.nn.relu(-across) + diffusion_number) * water[1:-1, :-2]
    moved = center + weight_down * (padded[:, :, 2:, 1:-1] - center)
    moved = moved + weight_up * (padded[:, :, :-2, 1:-1] - center)
    moved = moved + weight_right * (padded[:, :, 1:-1, 2:] - center)
    moved = moved + weight_left * (padded[:, :, 1:-1, :-2] - center)
    moved = moved * inner
    vertical_flux = mixing * (moved[:, 1:] - moved[:, :-1])
    zeros = jnp.zeros_like(moved[:, :1])
    return moved + jnp.concatenate([vertical_flux, zeros], 1) - jnp.concatenate([zeros, vertical_flux], 1)


def reference(adjoint_end, currents, plan, water_mask, mixing, decay, obs_weight, release_cells, profiles):
    water = jnp.pad(water_mask.astype(jnp.float32), 1)
    inner = water[1:-1, 1:-1]
    source = inner * adjoint_end
    keep = (1.0 - decay)[:, None, None, None]
    field = adjoint_end
    for hour_index in reversed(range(HOURS)):
        current = lax.dynamic_index_in_dim(currents, plan[hour_index], 0, keepdims=False)
        padded = jnp.pad(field, ((0, 0), (0, 0), (1, 1), (1, 1)))
        mixed = transport(padded, water, current, mixing)
        field = keep * mixed + obs_weight[hour_index][:, None, None, None] * source
    strips = field.reshape(RECEPTORS, LEVELS, NS, CX * NY)
    strip_ids = jnp.arange(NS, dtype=jnp.int32)[:, None, None]
    samples = strips[:, :, strip_ids, release_cells]
    samples = jnp.transpose(samples, (0, 2, 3, 1, 4)).reshape(RECEPTORS, NS, BLK_STRIP, LEVELS * CB)
    sensitivity = jnp.einsum("rsbk,sbkp->sbrp", samples, profiles, precision=lax.Precision.HIGHEST)
    return field, sensitivity
```

```python
import functools

import jax
import jax.numpy as jnp
from jax import lax
from jax.experimental import pallas as pl
from jax.experimental.pallas import tpu as pltpu
from jax.sharding import PartitionSpec as P

HOURS = 4
RIM = 4
LANES = 128


diffusion_number = 0.08


def transport_kernel(
    where_ref, cells_ref, keep_ref, obs_ref, adj_hbm, rim_hbm, water_hbm, mix_hbm,
    p0, p1, p2, p3, p4, p5, p6, p7,
    start_hbm, samples_hbm,
    strips, rims, field, source, water_in, water, masks, mix, cur, weights, table, picked, outgoing,
    sem_adj, sem_rim, sem_water, sem_mix, sem_cur, sem_out, sem_samples,
):
    levels, slots = field.shape[1], field.shape[2]
    tiles = strips.shape[0]
    own = slots - 2 * RIM
    recv = field.shape[3]
    x_here = where_ref[0]
    y_here = where_ref[1]

    copies = []
    for j in range(tiles):
        lanes = pl.ds(j * LANES, LANES)
        copies.append(pltpu.make_async_copy(adj_hbm.at[:, lanes], strips.at[j], sem_adj))
        copies.append(pltpu.make_async_copy(rim_hbm.at[:, lanes], rims.at[j], sem_rim))
    water_copy = pltpu.make_async_copy(water_hbm, water_in, sem_water)
    for j in range(tiles):
        lanes = pl.ds(j * LANES, LANES)
        copies.append(pltpu.make_async_copy(mix_hbm.at[:, :, lanes], mix.at[:, j, pl.ds(0, own)], sem_mix))
    for copy in copies:
        copy.start()
    water_copy.start()
    cur_copies = []
    for order, piece in enumerate((p0, p1, p2, p3, p4, p5, p6, p7)):
        dx, dy = order // 2, order % 2
        to = lax.rem(x_here + dx, 4) * 2 + (y_here + dy - 2 * y_here * dy)
        cur_copies.append(pltpu.make_async_copy(piece, cur.at[to], sem_cur))
    for copy in cur_copies:
        copy.start()
    for copy in copies:
        copy.wait()
    water_copy.wait()

    lane = lax.broadcasted_iota(jnp.int32, (8, LANES), 1)
    first = lane == 0
    last = lane == LANES - 1

    rim_first = levels * recv * 2 * RIM
    for j in range(tiles):
        lanes = slice(j * LANES, (j + 1) * LANES)
        for g in range(own // 8):
            water[j, 8 + g * 8:16 + g * 8, :] = water_in[g * 8:g * 8 + 8, lanes].astype(jnp.float32)
        water[j, 8 + own:8 + slots, :] = rims[j, rim_first:rim_first + 8, :]
        water[j, 7:8, :] = water[j, 7 + slots:8 + slots, :]
        water[j, 8 + slots:9 + slots, :] = water[j, 8:9, :]
        for k in range(levels - 1):
            mix[k, j, own:slots, :] = rims[j, rim_first + 8 * (k + 1):rim_first + 8 * (k + 2), :]

    def mask_rows(g, carry):
        base = pl.multiple_of(8 + g * 8, 8)
        here = [water[j, pl.ds(base, 8), :] for j in range(tiles)]
        right = [pltpu.roll(v, LANES - 1, 1) for v in here]
        left = [pltpu.roll(v, 1, 1) for v in here]
        rows = pl.ds(pl.multiple_of(g * 8, 8), 8)
        for j in range(tiles):
            masks[0, j, rows, :] = here[j]
            masks[1, j, rows, :] = here[j] * water[j, pl.ds(base + 1, 8), :]
            masks[2, j, rows, :] = here[j] * water[j, pl.ds(base - 1, 8), :]
            beyond = right[j + 1] if j + 1 < tiles else jnp.zeros_like(lane, jnp.float32)
            before = left[j - 1] if j > 0 else jnp.zeros_like(lane, jnp.float32)
            masks[3, j, rows, :] = here[j] * jnp.where(last, beyond, right[j])
            masks[4, j, rows, :] = here[j] * jnp.where(first, before, left[j])
        return carry

    lax.fori_loop(0, slots // 8, mask_rows, 0)

    def spread_own(row, carry):
        for j in range(tiles):
            lanes = slice(j * LANES, (j + 1) * LANES)
            wet = masks[0, j, pl.ds(row, 1), :]
            for l in range(levels):
                value = strips[j, pl.ds(l * own + row, recv, stride=levels * own), :]
                field[0, l, row, :, lanes] = value
                source[l, row, :, lanes] = wet * value
        return carry

    lax.fori_loop(0, own, spread_own, 0)

    def spread_rim(row, carry):
        for j in range(tiles):
            lanes = slice(j * LANES, (j + 1) * LANES)
            wet = masks[0, j, pl.ds(own + row, 1), :]
            for l in range(levels):
                value = rims[j, pl.ds(l * 2 * RIM + row, recv, stride=levels * 2 * RIM), :]
                field[0, l, own + row, :, lanes] = value
                source[l, own + row, :, lanes] = wet * value
        return carry

    lax.fori_loop(0, 2 * RIM, spread_rim, 0)

    for copy in cur_copies:
        copy.wait()

    keep = keep_ref[...]
    for step in range(HOURS):
        hour = HOURS - 1 - step

        def weigh(i, carry):
            g = lax.rem(i, slots // 8)
            l = i // (slots // 8)
            rows = pl.ds(pl.multiple_of(g * 8, 8), 8)
            for j in range(tiles):
                lanes = slice(j * LANES, (j + 1) * LANES)
                u = cur[l, hour, rows, lanes].astype(jnp.float32)
                v = cur[levels + l, hour, rows, lanes].astype(jnp.float32)
                down = (jnp.maximum(u, 0.0) + diffusion_number) * masks[1, j, rows, :]
                up = (jnp.maximum(-u, 0.0) + diffusion_number) * masks[2, j, rows, :]
                right = (jnp.maximum(v, 0.0) + diffusion_number) * masks[3, j, rows, :]
                left = (jnp.maximum(-v, 0.0) + diffusion_number) * masks[4, j, rows, :]
                weights[0, l, j, rows, :] = masks[0, j, rows, :] - ((down + up) + (right + left))
                weights[1, l, j, rows, :] = down
                weights[2, l, j, rows, :] = up
                weights[3, l, j, rows, :] = right
                weights[4, l, j, rows, :] = left
            return carry

        lax.fori_loop(0, levels * (slots // 8), weigh, 0)

        reach = HOURS - 1 - step
        old, new = step % 2, 1 - step % 2
        obs = obs_ref[hour]
        is_last = step == HOURS - 1

        def advance(i, carry):
            row = i - reach
            at = jnp.where(row < 0, row + slots, row)
            below = jnp.where(at == slots - 1, 0, at + 1)
            above = jnp.where(at == 0, slots - 1, at - 1)
            here = pl.ds(at, 1)
            value = [[None] * levels for _ in range(tiles + 1)]
            turn_r = [[None] * levels for _ in range(tiles + 1)]
            turn_l = [[None] * levels for _ in range(tiles + 1)]

            def fetch(j):
                lanes = slice(j * LANES, (j + 1) * LANES)
                for l in range(levels):
                    v = field[old, l, at, :, lanes]
                    value[j][l] = v
                    turn_r[j][l] = pltpu.roll(v, LANES - 1, 1)
                    turn_l[j][l] = pltpu.roll(v, 1, 1)

            fetch(0)
            for j in range(tiles):
                lanes = slice(j * LANES, (j + 1) * LANES)
                if j + 1 < tiles:
                    fetch(j + 1)
                moved = []
                for l in range(levels):
                    beyond = turn_r[j + 1][l] if j + 1 < tiles else turn_r[j][l]
                    before = turn_l[j - 1][l] if j > 0 else turn_l[j][l]
                    east = jnp.where(last, beyond, turn_r[j][l])
                    west = jnp.where(first, before, turn_l[j][l])
                    acc = weights[0, l, j, here, :] * value[j][l]
                    acc = acc + weights[1, l, j, here, :] * field[old, l, below, :, lanes]
                    acc = acc + weights[2, l, j, here, :] * field[old, l, above, :, lanes]
                    acc = acc + weights[3, l, j, here, :] * east
                    acc = acc + weights[4, l, j, here, :] * west
                    moved.append(acc)
                flux = [mix[k, j, here, :] * (moved[k + 1] - moved[k]) for k in range(levels - 1)]
                for l in range(levels):
                    mixed = moved[l]
                    if l < levels - 1:
                        mixed = mixed + flux[l]
                    if l > 0:
                        mixed = mixed - flux[l - 1]
                    result = keep * mixed + obs * source[l, at, :, lanes]
                    field[new, l, at, :, lanes] = result
                    if is_last:
                        strips[j, pl.ds(l * own + row, recv, stride=levels * own), :] = result
            return carry

        lax.fori_loop(0, own + 2 * reach, advance, 0)

    out_copies = [
        pltpu.make_async_copy(strips.at[j], start_hbm.at[:, pl.ds(j * LANES, LANES)], sem_out)
        for j in range(tiles)
    ]
    for copy in out_copies:
        copy.start()

    final = HOURS % 2

    def tabulate(row, carry):
        for j in range(tiles):
            lanes = slice(j * LANES, (j + 1) * LANES)
            stack = jnp.concatenate([field[final, l, row, :, lanes] for l in range(levels)], axis=0)
            stack = jnp.concatenate([stack] * (LANES // (levels * recv)), axis=0)
            at = pl.multiple_of((row * tiles + j) * LANES, LANES)
            table[pl.ds(at, LANES), :] = stack.T
        return carry

    lax.fori_loop(0, own, tabulate, 0)

    channels = levels * recv
    lane_row = lax.broadcasted_iota(jnp.int32, (1, LANES), 1)
    ways = LANES // channels

    def pick(g, carry):
        for c in range(LANES):
            value = table[pl.ds(cells_ref[g * ways, c], 1), :]
            for q in range(1, ways):
                other = table[pl.ds(cells_ref[g * ways + q, c], 1), :]
                value = jnp.where(lane_row < q * channels, value, other)
            picked[c:c + 1, :] = value
        outgoing[pl.ds(pl.multiple_of(g * LANES, LANES), LANES), :] = picked[...].T
        return carry

    lax.fori_loop(0, cells_ref.shape[0] // ways, pick, 0)
    samples_copy = pltpu.make_async_copy(outgoing, samples_hbm, sem_samples)
    samples_copy.start()
    samples_copy.wait()
    for copy in out_copies:
        copy.wait()


def response_kernel(samples_ref, profiles_ref, out_ref):
    batches, strips, channels, cells = samples_ref.shape
    levels = profiles_ref.shape[2] // cells
    recv = channels // levels
    for s in range(strips):
        total = None
        for l in range(levels):
            left = samples_ref[:, s, l * recv:(l + 1) * recv, :].reshape(batches * recv, cells)
            right = profiles_ref[s, 0, l * cells:(l + 1) * cells, :]
            part = jnp.dot(
                left, right, precision=lax.Precision.HIGHEST, preferred_element_type=jnp.float32
            )
            total = part if total is None else total + part
        out_ref[s, 0] = total


def rims_of(block, dim):
    count = lax.axis_size("space")
    forward = [(i, i + 1) for i in range(count - 1)]
    backward = [(b, a) for a, b in forward]
    size = block.shape[dim]
    low = lax.ppermute(lax.slice_in_dim(block, size - RIM, size, axis=dim), "space", forward)
    high = lax.ppermute(lax.slice_in_dim(block, 0, RIM, axis=dim), "space", backward)
    return jnp.concatenate([high, low], axis=dim)


def on_device(
    adjoint_end, currents, plan, water_mask, mixing, decay, obs_weight, release_cells, profiles
):
    recv, levels, own, width = adjoint_end.shape
    batches = lax.axis_size("rcpt")
    here = lax.axis_index("rcpt")
    x_count = batches // 2

    mine = currents[0]
    extended = jnp.concatenate([mine, rims_of(mine, 2)], axis=2)
    slots = own + 2 * RIM
    pieces = extended.reshape(batches, slots, width)
    pieces = lax.all_to_all(pieces, "rcpt", split_axis=0, concat_axis=0, tiled=True)
    wanted = jnp.take(pieces, plan, axis=0)
    across = [(i, i ^ 1) for i in range(batches)]
    partner = lax.ppermute(wanted, "rcpt", across)
    arrivals = [wanted, partner]
    for dx in range(1, x_count):
        route = [(i, (i - 2 * dx) % batches) for i in range(batches)]
        arrivals.append(lax.ppermute(wanted, "rcpt", route))
        arrivals.append(lax.ppermute(partner, "rcpt", route))

    edges = jnp.concatenate(
        [
            adjoint_end.reshape(recv * levels, own, width),
            water_mask.astype(jnp.float32)[None],
            mixing,
        ],
        axis=0,
    )
    rim = rims_of(edges, 1)
    rim = rim.reshape(-1, width)

    keep = jnp.broadcast_to((1.0 - decay)[:, None], (recv, LANES))
    obs = jnp.broadcast_to(obs_weight[:, :, None], (HOURS, recv, LANES))
    place = jnp.stack([here // 2, here % 2]).astype(jnp.int32)
    tiles = width // LANES
    blocks, cells = release_cells.shape[1:]
    channels = recv * levels
    hbm = pl.BlockSpec(memory_space=pl.ANY)
    smem = pl.BlockSpec(memory_space=pltpu.SMEM)
    vmem = pl.BlockSpec(memory_space=pltpu.VMEM)
    f32 = jnp.float32
    start, samples = pl.pallas_call(
        transport_kernel,
        out_shape=(
            jax.ShapeDtypeStruct((channels * own, width), f32),
            jax.ShapeDtypeStruct((blocks * channels, cells), f32),
        ),
        in_specs=[smem, smem, vmem, vmem] + [hbm] * 12,
        out_specs=(hbm, hbm),
        scratch_shapes=[
            pltpu.VMEM((tiles, channels * own, LANES), f32),
            pltpu.VMEM((tiles, (channels + levels) * 2 * RIM, LANES), f32),
            pltpu.VMEM((2, levels, slots, recv, width), f32),
            pltpu.VMEM((levels, slots, recv, width), f32),
            pltpu.VMEM((own, width), jnp.int32),
            pltpu.VMEM((tiles, slots + 16, LANES), f32),
            pltpu.VMEM((5, tiles, slots, LANES), f32),
            pltpu.VMEM((levels - 1, tiles, slots, LANES), f32),
            pltpu.VMEM((2 * levels, HOURS, slots, width), jnp.bfloat16),
            pltpu.VMEM((5, levels, tiles, slots, LANES), f32),
            pltpu.VMEM((own * width, LANES), f32),
            pltpu.VMEM((cells, LANES), f32),
            pltpu.VMEM((blocks * channels, cells), f32),
        ]
        + [pltpu.SemaphoreType.DMA] * 7,
        compiler_params=pltpu.CompilerParams(vmem_limit_bytes=67_000_000),
        name="transport",
    )(
        place, release_cells[0], keep, obs,
        adjoint_end.reshape(channels * own, width), rim, water_mask, mixing, *arrivals,
    )
    sending = samples.reshape(blocks, channels, cells)
    gathered = lax.all_to_all(sending, ("rcpt", "space"), split_axis=0, concat_axis=0, tiled=True)
    strips = lax.axis_size("space")
    gathered = gathered.reshape(batches, strips, channels, cells)
    group = 4
    own_blocks, depth, scenarios = profiles.shape[1:]
    result = pl.pallas_call(
        response_kernel,
        grid=(strips // group,),
        out_shape=jax.ShapeDtypeStruct((strips, own_blocks, batches * recv, scenarios), f32),
        in_specs=[
            pl.BlockSpec((batches, group, channels, cells), lambda s: (0, s, 0, 0)),
            pl.BlockSpec((group, own_blocks, depth, scenarios), lambda s: (s, 0, 0, 0)),
        ],
        out_specs=pl.BlockSpec((group, own_blocks, batches * recv, scenarios), lambda s: (s, 0, 0, 0)),
        name="response",
    )(gathered, profiles)
    return (start.reshape(recv, levels, own, width), result)


def solution(mesh):
    placed = (
        P("rcpt", None, "space", None),
        P("rcpt", None, None, "space", None),
        P(),
        P("space", None),
        P(None, "space", None),
        P("rcpt"),
        P(None, "rcpt"),
        P("space", None, None),
        P(None, ("rcpt", "space"), None, None),
    )
    return jax.shard_map(
        on_device,
        mesh=mesh,
        in_specs=placed,
        out_specs=(P("rcpt", None, "space", None), P(None, ("rcpt", "space"), None, None)),
        check_vma=False,
    )
```

```python
import functools

import jax
import jax.numpy as jnp
from jax import lax
from jax.experimental import pallas as pl
from jax.experimental.pallas import tpu as pltpu
from jax.sharding import PartitionSpec as P


HOURS = 4
RIM = 4
LANES = 128


diffusion_number = 0.08


def transport_kernel(
    decay_ref, obs_ref, cells_hbm, adj_hbm, rim_hbm, water_hbm, mix_hbm,
    p0, p1, p2, p3, q0, q1, q2, q3,
    start_hbm, samples_hbm,
    origin, field_a, field_b, water_in, water, masks, mix, cur, weights, table, picked, outgoing,
    cell_slots, sem_in, sem_origin, sem_cur, sem_out, sem_samples, sem_cells,
):
    levels, slots, recv, _ = origin.shape
    tiles = water.shape[0]
    own = slots - 2 * RIM
    x_here = lax.axis_index("rcpt") // 2
    depth = p0.shape[1]
    cur_copies = []
    for dx, (piece, piece_rim) in enumerate(((p0, q0), (p1, q1), (p2, q2), (p3, q3))):
        to = pl.ds(lax.rem(x_here + dx, 4) * depth, depth)
        cur_copies.append(pltpu.make_async_copy(piece, cur.at[:, to, pl.ds(0, own)], sem_cur))
        cur_copies.append(
            pltpu.make_async_copy(piece_rim, cur.at[pl.ds(1, HOURS - 1), to, pl.ds(own, 2 * RIM)], sem_cur)
        )

    copies = [pltpu.make_async_copy(water_hbm, water_in, sem_in)]
    for j in range(tiles):
        lanes = pl.ds(j * LANES, LANES)
        copies.append(pltpu.make_async_copy(mix_hbm.at[:, :, lanes], mix.at[:, j, pl.ds(0, own)], sem_in))
        copies.append(
            pltpu.make_async_copy(
                rim_hbm.at[pl.ds(levels * recv + 1, levels - 1), :, lanes],
                mix.at[:, j, pl.ds(own, 2 * RIM)],
                sem_in,
            )
        )
        copies.append(
            pltpu.make_async_copy(
                rim_hbm.at[levels * recv, :, lanes], water.at[j, pl.ds(8 + own, 2 * RIM)], sem_in
            )
        )
    origin_copies = []
    for r in range(recv):
        origin_copies.append(
            pltpu.make_async_copy(adj_hbm.at[r], origin.at[:, pl.ds(0, own), r, :], sem_origin)
        )
        origin_copies.append(
            pltpu.make_async_copy(
                rim_hbm.at[pl.ds(r * levels, levels)],
                origin.at[:, pl.ds(own, 2 * RIM), r, :],
                sem_origin,
            )
        )
    for copy in copies + cur_copies + origin_copies:
        copy.start()

    def cells_copy(i, slot):
        return pltpu.make_async_copy(
            cells_hbm.at[pl.ds(i * 8, 8)], cell_slots.at[slot], sem_cells.at[slot]
        )

    cell_ring = cell_slots.shape[0]
    for slot in range(cell_ring):
        cells_copy(slot, slot).start()
    for copy in copies:
        copy.wait()

    lane = lax.broadcasted_iota(jnp.int32, (8, LANES), 1)
    first = lane == 0
    last = lane == LANES - 1

    for j in range(tiles):
        lanes = slice(j * LANES, (j + 1) * LANES)
        for g in range(own // 8):
            water[j, 8 + g * 8:16 + g * 8, :] = water_in[g * 8:g * 8 + 8, lanes].astype(jnp.float32)
        water[j, 7:8, :] = water[j, 7 + slots:8 + slots, :]
        water[j, 8 + slots:9 + slots, :] = water[j, 8:9, :]

    def mask_rows(g, carry):
        base = pl.multiple_of(8 + g * 8, 8)
        here = [water[j, pl.ds(base, 8), :] for j in range(tiles)]
        right = [pltpu.roll(v, LANES - 1, 1) for v in here]
        left = [pltpu.roll(v, 1, 1) for v in here]
        rows = pl.ds(pl.multiple_of(g * 8, 8), 8)
        for j in range(tiles):
            masks[0, j, rows, :] = here[j]
            masks[1, j, rows, :] = here[j] * water[j, pl.ds(base + 1, 8), :]
            masks[2, j, rows, :] = here[j] * water[j, pl.ds(base - 1, 8), :]
            beyond = right[j + 1] if j + 1 < tiles else jnp.zeros_like(lane, jnp.float32)
            before = left[j - 1] if j > 0 else jnp.zeros_like(lane, jnp.float32)
            masks[3, j, rows, :] = here[j] * jnp.where(last, beyond, right[j])
            masks[4, j, rows, :] = here[j] * jnp.where(first, before, left[j])
        return carry

    lax.fori_loop(0, slots // 8, mask_rows, 0)

    for copy in cur_copies:
        copy.wait()

    sublane = lax.broadcasted_iota(jnp.int32, (recv, LANES), 0)

    def per_receptor(read):
        spread = jnp.zeros((recv, LANES), jnp.float32)
        for r in range(recv):
            spread = jnp.where(sublane == r, read(r), spread)
        return spread

    keep = per_receptor(lambda r: 1.0 - decay_ref[r])
    for step in range(HOURS):
        hour = HOURS - 1 - step

        def weigh(i, carry):
            g = lax.rem(i, slots // 8)
            l = i // (slots // 8)
            rows = pl.ds(pl.multiple_of(g * 8, 8), 8)
            for j in range(tiles):
                lanes = slice(j * LANES, (j + 1) * LANES)
                u = cur[hour, l, rows, lanes].astype(jnp.float32)
                v = cur[hour, levels + l, rows, lanes].astype(jnp.float32)
                down = (jnp.maximum(u, 0.0) + diffusion_number) * masks[1, j, rows, :]
                up = (jnp.maximum(-u, 0.0) + diffusion_number) * masks[2, j, rows, :]
                right = (jnp.maximum(v, 0.0) + diffusion_number) * masks[3, j, rows, :]
                left = (jnp.maximum(-v, 0.0) + diffusion_number) * masks[4, j, rows, :]
                weights[0, l, j, rows, :] = masks[0, j, rows, :] - ((down + up) + (right + left))
                weights[1, l, j, rows, :] = down
                weights[2, l, j, rows, :] = up
                weights[3, l, j, rows, :] = right
                weights[4, l, j, rows, :] = left
            return carry

        lax.fori_loop(0, levels * (slots // 8), weigh, 0, unroll=2)
        if step == 0:
            for copy in origin_copies:
                copy.wait()

        reach = HOURS - 1 - step
        old = (origin, field_a, field_b, field_a)[step]
        new = (field_a, field_b, field_a, field_b)[step]
        obs = per_receptor(lambda r: obs_ref[hour, r])

        def advance(i, carry):
            row = i - reach
            at = jnp.where(row < 0, row + slots, row)
            below = jnp.where(at == slots - 1, 0, at + 1)
            above = jnp.where(at == 0, slots - 1, at - 1)
            here = pl.ds(at, 1)
            value = [[None] * levels for _ in range(tiles)]
            turn_r = [[None] * levels for _ in range(tiles)]
            turn_l = [[None] * levels for _ in range(tiles)]

            def fetch(j):
                lanes = slice(j * LANES, (j + 1) * LANES)
                for l in range(levels):
                    v = old[l, at, :, lanes]
                    value[j][l] = v
                    turn_r[j][l] = pltpu.roll(v, LANES - 1, 1)
                    turn_l[j][l] = pltpu.roll(v, 1, 1)

            fetch(0)
            for j in range(tiles):
                lanes = slice(j * LANES, (j + 1) * LANES)
                if j + 1 < tiles:
                    fetch(j + 1)
                forced = obs * masks[0, j, here, :]
                moved = []
                for l in range(levels):
                    beyond = turn_r[j + 1][l] if j + 1 < tiles else turn_r[j][l]
                    before = turn_l[j - 1][l] if j > 0 else turn_l[j][l]
                    east = jnp.where(last, beyond, turn_r[j][l])
                    west = jnp.where(first, before, turn_l[j][l])
                    acc = weights[0, l, j, here, :] * value[j][l]
                    acc = acc + weights[1, l, j, here, :] * old[l, below, :, lanes]
                    acc = acc + weights[2, l, j, here, :] * old[l, above, :, lanes]
                    acc = acc + weights[3, l, j, here, :] * east
                    acc = acc + weights[4, l, j, here, :] * west
                    moved.append(acc)
                flux = [mix[k, j, here, :] * (moved[k + 1] - moved[k]) for k in range(levels - 1)]
                for l in range(levels):
                    mixed = moved[l]
                    if l < levels - 1:
                        mixed = mixed + flux[l]
                    if l > 0:
                        mixed = mixed - flux[l - 1]
                    result = keep * mixed + forced * origin[l, at, :, lanes]
                    new[l, at, :, lanes] = result
            return carry

        lax.fori_loop(0, own + 2 * reach, advance, 0, unroll=2)

    out_copies = [
        pltpu.make_async_copy(field_b.at[:, pl.ds(0, own), r, :], start_hbm.at[r], sem_out)
        for r in range(recv)
    ]
    for copy in out_copies:
        copy.start()

    def tabulate(row, carry):
        for j in range(tiles):
            lanes = slice(j * LANES, (j + 1) * LANES)
            stack = jnp.concatenate([field_b[l, row, :, lanes] for l in range(levels)], axis=0)
            at = pl.multiple_of((row * tiles + j) * LANES, LANES)
            table[pl.ds(at, LANES), :] = stack.T
        return carry

    lax.fori_loop(0, own, tabulate, 0)

    channels = levels * recv
    blocks = cells_hbm.shape[0]
    rounds = blocks // 8 // cell_ring

    def samples_copy(i, slot):
        at = pl.ds(pl.multiple_of((i * cell_ring + slot) * 8 * channels, 8 * channels), 8 * channels)
        return pltpu.make_async_copy(outgoing.at[at], samples_hbm.at[at], sem_samples)

    def pick(i, carry):
        for slot in range(cell_ring):
            cells_copy(i * cell_ring + slot, slot).wait()
            for k in range(8):
                for c in range(LANES):
                    picked[k % 4, c:c + 1, :] = table[pl.ds(cell_slots[slot, k, c], 1), :]
                at = pl.multiple_of(((i * cell_ring + slot) * 8 + k) * channels, channels)
                outgoing[pl.ds(at, channels), :] = picked[k % 4].T
            samples_copy(i, slot).start()

            @pl.when(i + 1 < rounds)
            def _():
                cells_copy((i + 1) * cell_ring + slot, slot).start()
        return carry

    lax.fori_loop(0, rounds, pick, 0)
    for copy in out_copies:
        copy.wait()
    pltpu.make_async_copy(outgoing, samples_hbm, sem_samples).wait()


def response_kernel(samples_ref, profiles_ref, out_ref):
    batches, strips, channels, cells = samples_ref.shape
    levels = profiles_ref.shape[2] // cells
    recv = channels // levels
    for s in range(strips):
        total = None
        for l in range(levels):
            left = samples_ref[:, s, l * recv:(l + 1) * recv, :].reshape(batches * recv, cells)
            right = profiles_ref[s, 0, l * cells:(l + 1) * cells, :]
            part = jnp.dot(
                left, right, precision=lax.Precision.HIGHEST, preferred_element_type=jnp.float32
            )
            total = part if total is None else total + part
        out_ref[s, 0] = total


def shift_rims(upper, lower, dim):
    count = lax.axis_size("space")
    forward = [(i, i + 1) for i in range(count - 1)]
    backward = [(b, a) for a, b in forward]
    low = lax.ppermute(upper, "space", forward)
    high = lax.ppermute(lower, "space", backward)
    return jnp.concatenate([high, low], axis=dim)


def on_device(
    adjoint_end, currents, plan, water_mask, mixing, decay, obs_weight, release_cells, profiles
):
    recv, levels, own, width = adjoint_end.shape
    batches = lax.axis_size("rcpt")
    x_count = batches // 2
    slots = own + 2 * RIM

    pieces = currents.reshape(x_count, 1, -1, own, width)
    depth = pieces.shape[2]
    pieces = jnp.broadcast_to(pieces, (x_count, 2, depth, own, width)).reshape(batches, depth, own, width)
    with jax.named_scope("spread"):
        pieces = lax.all_to_all(pieces, "rcpt", split_axis=0, concat_axis=0, tiled=True)
    wanted = jnp.take(pieces, plan, axis=0, mode="clip")
    routes = [[(i, (i - 2 * dx) % batches) for i in range(batches)] for dx in range(1, x_count)]
    with jax.named_scope("gather"):
        arrivals = [wanted] + [lax.ppermute(wanted, "rcpt", route) for route in routes]
    with jax.named_scope("cur_rim"):
        cur_rim = shift_rims(wanted[1:, :, own - RIM:], wanted[1:, :, :RIM], 2)
        arrivals += [cur_rim] + [lax.ppermute(cur_rim, "rcpt", route) for route in routes]

    edges = jnp.concatenate(
        [
            adjoint_end.reshape(recv * levels, own, width),
            water_mask.astype(jnp.float32)[None],
            mixing,
        ],
        axis=0,
    )
    with jax.named_scope("field_rim"):
        rim = shift_rims(edges[:, own - RIM:], edges[:, :RIM], 1)

    tiles = width // LANES
    blocks, cells = release_cells.shape[1:]
    channels = recv * levels
    hbm = pl.BlockSpec(memory_space=pl.ANY)
    smem = pl.BlockSpec(memory_space=pltpu.SMEM)
    f32 = jnp.float32
    start, samples = pl.pallas_call(
        transport_kernel,
        out_shape=(
            jax.ShapeDtypeStruct((recv, levels, own, width), f32),
            jax.ShapeDtypeStruct((blocks * channels, cells), f32),
        ),
        in_specs=[smem, smem] + [hbm] * 13,
        out_specs=(hbm, hbm),
        scratch_shapes=[
            pltpu.VMEM((levels, slots, recv, width), f32),
            pltpu.VMEM((levels, slots, recv, width), f32),
            pltpu.VMEM((levels, slots, recv, width), f32),
            pltpu.VMEM((own, width), jnp.int32),
            pltpu.VMEM((tiles, slots + 16, LANES), f32),
            pltpu.VMEM((5, tiles, slots, LANES), f32),
            pltpu.VMEM((levels - 1, tiles, slots, LANES), f32),
            pltpu.VMEM((HOURS, 2 * levels, slots, width), jnp.bfloat16),
            pltpu.VMEM((5, levels, tiles, slots, LANES), f32),
            pltpu.VMEM((own * width, channels), f32),
            pltpu.VMEM((4, cells, channels), f32),
            pltpu.VMEM((blocks * channels, cells), f32),
            pltpu.SMEM((4, 8, cells), jnp.int32),
        ]
        + [pltpu.SemaphoreType.DMA] * 5
        + [pltpu.SemaphoreType.DMA((4,))],
        compiler_params=pltpu.CompilerParams(vmem_limit_bytes=67_000_000),
        name="transport",
    )(decay, obs_weight, release_cells[0], adjoint_end, rim, water_mask, mixing, *arrivals)
    sending = samples.reshape(blocks, channels, cells)
    gathered = lax.all_to_all(sending, ("rcpt", "space"), split_axis=0, concat_axis=0, tiled=True)
    strips = lax.axis_size("space")
    gathered = gathered.reshape(batches, strips, channels, cells)
    group = 4
    own_blocks, depth, scenarios = profiles.shape[1:]
    result = pl.pallas_call(
        response_kernel,
        grid=(strips // group,),
        out_shape=jax.ShapeDtypeStruct((strips, own_blocks, batches * recv, scenarios), f32),
        in_specs=[
            pl.BlockSpec((batches, group, channels, cells), lambda s: (0, s, 0, 0)),
            pl.BlockSpec((group, own_blocks, depth, scenarios), lambda s: (s, 0, 0, 0)),
        ],
        out_specs=pl.BlockSpec((group, own_blocks, batches * recv, scenarios), lambda s: (s, 0, 0, 0)),
        compiler_params=pltpu.CompilerParams(vmem_limit_bytes=16_000_000),
        name="response",
    )(gathered, profiles)
    return (start, result)


def solution(mesh):
    placed = (
        P("rcpt", None, "space", None),
        P("rcpt", None, None, "space", None),
        P(),
        P("space", None),
        P(None, "space", None),
        P("rcpt"),
        P(None, "rcpt"),
        P("space", None, None),
        P(None, ("rcpt", "space"), None, None),
    )
    return jax.shard_map(
        on_device,
        mesh=mesh,
        in_specs=placed,
        out_specs=(P("rcpt", None, "space", None), P(None, ("rcpt", "space"), None, None)),
        check_vma=False,
    )
```

```python
import functools

import jax
import jax.numpy as jnp
from jax import lax
from jax.experimental import pallas as pl
from jax.experimental.pallas import tpu as pltpu
from jax.sharding import PartitionSpec as P


HOURS = 4
RIM = 4
LANES = 128


diffusion_number = 0.08


SCALE_STEPS = 64
LARGEST = 32700.0


def encode(samples, recv):
    channels, cells = samples.shape
    levels = channels // recv
    reach = jnp.maximum(jnp.max(jnp.abs(samples), axis=1, keepdims=True), 1e-30)
    power = jnp.ceil(jnp.log2(reach) * SCALE_STEPS)
    codes = jnp.round(samples * (LARGEST * jnp.exp2(power * (-1.0 / SCALE_STEPS))))
    part = lax.broadcasted_iota(jnp.int32, (recv, cells), 1) // (cells // levels)
    powers = jnp.broadcast_to(power[:recv], (recv, cells))
    for l in range(1, levels):
        powers = jnp.where(part == l, power[l * recv:(l + 1) * recv], powers)
    return jnp.concatenate([codes, powers], axis=0).astype(jnp.int32).astype(jnp.int16)


def transport_kernel(
    decay_ref, obs_ref, cells_hbm, adj_hbm, rim_hbm, water_hbm, mix_hbm,
    p0, p1, p2, p3, q0, q1, q2, q3,
    start_hbm, samples_hbm,
    origin, field_a, field_b, water_in, water, masks, mix, cur, weights, table, picked, outgoing,
    cell_slots, sem_in, sem_origin, sem_cur, sem_out, sem_samples, sem_cells,
):
    levels, slots, recv, _ = origin.shape
    tiles = water.shape[0]
    own = slots - 2 * RIM
    x_here = lax.axis_index("rcpt") // 2
    depth = p0.shape[1]
    cur_copies = []
    for dx, (piece, piece_rim) in enumerate(((p0, q0), (p1, q1), (p2, q2), (p3, q3))):
        to = pl.ds(lax.rem(x_here + dx, 4) * depth, depth)
        cur_copies.append(pltpu.make_async_copy(piece, cur.at[:, to, pl.ds(0, own)], sem_cur))
        cur_copies.append(
            pltpu.make_async_copy(piece_rim, cur.at[pl.ds(1, HOURS - 1), to, pl.ds(own, 2 * RIM)], sem_cur)
        )

    copies = [pltpu.make_async_copy(water_hbm, water_in, sem_in)]
    for j in range(tiles):
        lanes = pl.ds(j * LANES, LANES)
        copies.append(pltpu.make_async_copy(mix_hbm.at[:, :, lanes], mix.at[:, j, pl.ds(0, own)], sem_in))
        copies.append(
            pltpu.make_async_copy(
                rim_hbm.at[pl.ds(levels * recv + 1, levels - 1), :, lanes],
                mix.at[:, j, pl.ds(own, 2 * RIM)],
                sem_in,
            )
        )
        copies.append(
            pltpu.make_async_copy(
                rim_hbm.at[levels * recv, :, lanes], water.at[j, pl.ds(8 + own, 2 * RIM)], sem_in
            )
        )
    origin_copies = []
    for r in range(recv):
        origin_copies.append(
            pltpu.make_async_copy(adj_hbm.at[r], origin.at[:, pl.ds(0, own), r, :], sem_origin)
        )
        origin_copies.append(
            pltpu.make_async_copy(
                rim_hbm.at[pl.ds(r * levels, levels)],
                origin.at[:, pl.ds(own, 2 * RIM), r, :],
                sem_origin,
            )
        )
    for copy in copies + cur_copies + origin_copies:
        copy.start()

    cell_ring, held, _ = cell_slots.shape

    def cells_copy(i, slot):
        return pltpu.make_async_copy(
            cells_hbm.at[pl.ds(i * held, held)], cell_slots.at[slot], sem_cells.at[slot]
        )

    for slot in range(cell_ring):
        cells_copy(slot, slot).start()
    for copy in copies:
        copy.wait()

    lane = lax.broadcasted_iota(jnp.int32, (8, LANES), 1)
    first = lane == 0
    last = lane == LANES - 1

    for j in range(tiles):
        lanes = slice(j * LANES, (j + 1) * LANES)
        for g in range(own // 8):
            water[j, 8 + g * 8:16 + g * 8, :] = water_in[g * 8:g * 8 + 8, lanes].astype(jnp.float32)
        water[j, 7:8, :] = water[j, 7 + slots:8 + slots, :]
        water[j, 8 + slots:9 + slots, :] = water[j, 8:9, :]

    def mask_rows(g, carry):
        base = pl.multiple_of(8 + g * 8, 8)
        here = [water[j, pl.ds(base, 8), :] for j in range(tiles)]
        right = [pltpu.roll(v, LANES - 1, 1) for v in here]
        left = [pltpu.roll(v, 1, 1) for v in here]
        rows = pl.ds(pl.multiple_of(g * 8, 8), 8)
        for j in range(tiles):
            masks[0, j, rows, :] = here[j]
            masks[1, j, rows, :] = here[j] * water[j, pl.ds(base + 1, 8), :]
            masks[2, j, rows, :] = here[j] * water[j, pl.ds(base - 1, 8), :]
            beyond = right[j + 1] if j + 1 < tiles else jnp.zeros_like(lane, jnp.float32)
            before = left[j - 1] if j > 0 else jnp.zeros_like(lane, jnp.float32)
            masks[3, j, rows, :] = here[j] * jnp.where(last, beyond, right[j])
            masks[4, j, rows, :] = here[j] * jnp.where(first, before, left[j])
        return carry

    lax.fori_loop(0, slots // 8, mask_rows, 0)

    for copy in cur_copies:
        copy.wait()

    sublane = lax.broadcasted_iota(jnp.int32, (recv, LANES), 0)

    def per_receptor(read):
        spread = jnp.zeros((recv, LANES), jnp.float32)
        for r in range(recv):
            spread = jnp.where(sublane == r, read(r), spread)
        return spread

    keep = per_receptor(lambda r: 1.0 - decay_ref[r])
    for step in range(HOURS):
        hour = HOURS - 1 - step

        def weigh(i, carry):
            g = lax.rem(i, slots // 8)
            l = i // (slots // 8)
            rows = pl.ds(pl.multiple_of(g * 8, 8), 8)
            for j in range(tiles):
                lanes = slice(j * LANES, (j + 1) * LANES)
                u = cur[hour, l, rows, lanes].astype(jnp.float32)
                v = cur[hour, levels + l, rows, lanes].astype(jnp.float32)
                down = (jnp.maximum(u, 0.0) + diffusion_number) * masks[1, j, rows, :]
                up = (jnp.maximum(-u, 0.0) + diffusion_number) * masks[2, j, rows, :]
                right = (jnp.maximum(v, 0.0) + diffusion_number) * masks[3, j, rows, :]
                left = (jnp.maximum(-v, 0.0) + diffusion_number) * masks[4, j, rows, :]
                weights[0, l, j, rows, :] = masks[0, j, rows, :] - ((down + up) + (right + left))
                weights[1, l, j, rows, :] = down
                weights[2, l, j, rows, :] = up
                weights[3, l, j, rows, :] = right
                weights[4, l, j, rows, :] = left
            return carry

        lax.fori_loop(0, levels * (slots // 8), weigh, 0, unroll=2)
        if step == 0:
            for copy in origin_copies:
                copy.wait()

        reach = HOURS - 1 - step
        old = (origin, field_a, field_b, field_a)[step]
        new = (field_a, field_b, field_a, field_b)[step]
        kept = keep if step == 0 else kept * keep
        obs = per_receptor(lambda r: obs_ref[hour, r]) / kept
        is_last = step == HOURS - 1

        def advance(i, carry):
            row = i - reach
            at = jnp.where(row < 0, row + slots, row)
            below = jnp.where(at == slots - 1, 0, at + 1)
            above = jnp.where(at == 0, slots - 1, at - 1)
            here = pl.ds(at, 1)
            value = [[None] * levels for _ in range(tiles)]
            turn_r = [[None] * levels for _ in range(tiles)]
            turn_l = [[None] * levels for _ in range(tiles)]

            def fetch(j):
                lanes = slice(j * LANES, (j + 1) * LANES)
                for l in range(levels):
                    v = old[l, at, :, lanes]
                    value[j][l] = v
                    turn_r[j][l] = pltpu.roll(v, LANES - 1, 1)
                    turn_l[j][l] = pltpu.roll(v, 1, 1)

            fetch(0)
            for j in range(tiles):
                lanes = slice(j * LANES, (j + 1) * LANES)
                if j + 1 < tiles:
                    fetch(j + 1)
                forced = obs * masks[0, j, here, :]
                moved = []
                for l in range(levels):
                    beyond = turn_r[j + 1][l] if j + 1 < tiles else turn_r[j][l]
                    before = turn_l[j - 1][l] if j > 0 else turn_l[j][l]
                    east = jnp.where(last, beyond, turn_r[j][l])
                    west = jnp.where(first, before, turn_l[j][l])
                    acc = weights[0, l, j, here, :] * value[j][l]
                    acc = acc + weights[1, l, j, here, :] * old[l, below, :, lanes]
                    acc = acc + weights[2, l, j, here, :] * old[l, above, :, lanes]
                    acc = acc + weights[3, l, j, here, :] * east
                    acc = acc + weights[4, l, j, here, :] * west
                    moved.append(acc)
                flux = [mix[k, j, here, :] * (moved[k + 1] - moved[k]) for k in range(levels - 1)]
                results = []
                for l in range(levels):
                    mixed = moved[l]
                    if l < levels - 1:
                        mixed = mixed + flux[l]
                    if l > 0:
                        mixed = mixed - flux[l - 1]
                    result = mixed + forced * origin[l, at, :, lanes]
                    if is_last:
                        result = kept * result
                    results.append(result)
                    new[l, at, :, lanes] = result
            return carry

        lax.fori_loop(0, own + 2 * reach, advance, 0, unroll=4 if (own + 2 * reach) % 4 == 0 else 2)

    out_copies = [
        pltpu.make_async_copy(field_b.at[:, pl.ds(0, own), r, :], start_hbm.at[r], sem_out)
        for r in range(recv)
    ]
    for copy in out_copies:
        copy.start()

    def tabulate(row, carry):
        for j in range(tiles):
            lanes = slice(j * LANES, (j + 1) * LANES)
            stack = jnp.concatenate([field_b[l, row, :, lanes] for l in range(levels)], axis=0)
            at = pl.multiple_of((row * tiles + j) * LANES, LANES)
            table[pl.ds(at, LANES), :] = stack.T
        return carry

    lax.fori_loop(0, own, tabulate, 0, unroll=4)

    channels = levels * recv
    blocks = cells_hbm.shape[0]
    rounds = blocks // held // cell_ring

    def samples_copy(i, slot):
        at = pl.ds((i * cell_ring + slot) * held, held)
        return pltpu.make_async_copy(outgoing.at[at], samples_hbm.at[at], sem_samples)

    def pick(i, carry):
        for slot in range(cell_ring):
            cells_copy(i * cell_ring + slot, slot).wait()
            for k in range(held):
                for c in range(LANES):
                    picked[k % 4, c:c + 1, :] = table[pl.ds(cell_slots[slot, k, c], 1), :]
                outgoing[(i * cell_ring + slot) * held + k] = encode(picked[k % 4].T, recv)
            samples_copy(i, slot).start()
            cells_copy(jnp.minimum(i + 1, rounds - 1) * cell_ring + slot, slot).start()
        return carry

    lax.fori_loop(0, rounds, pick, 0)
    for slot in range(cell_ring):
        cells_copy(slot, slot).wait()
    for copy in out_copies:
        copy.wait()
    pltpu.make_async_copy(outgoing, samples_hbm, sem_samples).wait()


def response_kernel(samples_ref, profiles_ref, out_ref):
    batches, strips, rows, cells = samples_ref.shape
    levels = profiles_ref.shape[2] // cells
    recv = rows // (levels + 1)
    for s in range(strips):
        coded = samples_ref[:, s].astype(jnp.int32).astype(jnp.float32)
        scales = jnp.exp2(coded[:, levels * recv:] * (1.0 / SCALE_STEPS)) * (1.0 / LARGEST)
        total = None
        for l in range(levels):
            lane = l * (cells // levels)
            left = coded[:, l * recv:(l + 1) * recv] * scales[:, :, lane:lane + 1]
            part = jnp.dot(
                left.reshape(batches * recv, cells),
                profiles_ref[s, 0, l * cells:(l + 1) * cells, :],
                precision=lax.Precision.HIGHEST,
                preferred_element_type=jnp.float32,
            )
            total = part if total is None else total + part
        out_ref[s, 0] = total


def shift_rims(upper, lower, dim):
    count = lax.axis_size("space")
    forward = [(i, i + 1) for i in range(count - 1)]
    backward = [(b, a) for a, b in forward]
    low = lax.ppermute(upper, "space", forward)
    high = lax.ppermute(lower, "space", backward)
    return jnp.concatenate([high, low], axis=dim)


def on_device(
    adjoint_end, currents, plan, water_mask, mixing, decay, obs_weight, release_cells, profiles
):
    recv, levels, own, width = adjoint_end.shape
    batches = lax.axis_size("rcpt")
    x_count = batches // 2
    slots = own + 2 * RIM

    pieces = currents.reshape(x_count, 1, -1, own, width)
    depth = pieces.shape[2]
    pieces = jnp.broadcast_to(pieces, (x_count, 2, depth, own, width)).reshape(batches, depth, own, width)
    with jax.named_scope("spread"):
        pieces = lax.all_to_all(pieces, "rcpt", split_axis=0, concat_axis=0, tiled=True)
    wanted = jnp.take(pieces, plan, axis=0, mode="clip")
    routes = [[(i, (i - 2 * dx) % batches) for i in range(batches)] for dx in range(1, x_count)]
    with jax.named_scope("gather"):
        arrivals = [wanted] + [lax.ppermute(wanted, "rcpt", route) for route in routes]
    with jax.named_scope("cur_rim"):
        cur_rim = shift_rims(wanted[1:, :, own - RIM:], wanted[1:, :, :RIM], 2)
        arrivals += [cur_rim] + [lax.ppermute(cur_rim, "rcpt", route) for route in routes]

    edges = jnp.concatenate(
        [
            adjoint_end.reshape(recv * levels, own, width),
            water_mask.astype(jnp.float32)[None],
            mixing,
        ],
        axis=0,
    )
    with jax.named_scope("field_rim"):
        rim = shift_rims(edges[:, own - RIM:], edges[:, :RIM], 1)

    tiles = width // LANES
    blocks, cells = release_cells.shape[1:]
    channels = recv * levels
    hbm = pl.BlockSpec(memory_space=pl.ANY)
    smem = pl.BlockSpec(memory_space=pltpu.SMEM)
    f32 = jnp.float32
    start, samples = pl.pallas_call(
        transport_kernel,
        out_shape=(
            jax.ShapeDtypeStruct((recv, levels, own, width), f32),
            jax.ShapeDtypeStruct((blocks, channels + recv, cells), jnp.int16),
        ),
        in_specs=[smem, smem] + [hbm] * 13,
        out_specs=(hbm, hbm),
        scratch_shapes=[
            pltpu.VMEM((levels, slots, recv, width), f32),
            pltpu.VMEM((levels, slots, recv, width), f32),
            pltpu.VMEM((levels, slots, recv, width), f32),
            pltpu.VMEM((own, width), jnp.int32),
            pltpu.VMEM((tiles, slots + 16, LANES), f32),
            pltpu.VMEM((5, tiles, slots, LANES), f32),
            pltpu.VMEM((levels - 1, tiles, slots, LANES), f32),
            pltpu.VMEM((HOURS, 2 * levels, slots, width), jnp.bfloat16),
            pltpu.VMEM((5, levels, tiles, slots, LANES), f32),
            pltpu.VMEM((own * width, channels), f32),
            pltpu.VMEM((4, cells, channels), f32),
            pltpu.VMEM((blocks, channels + recv, cells), jnp.int16),
            pltpu.SMEM((2, 16, cells), jnp.int32),
        ]
        + [pltpu.SemaphoreType.DMA] * 5
        + [pltpu.SemaphoreType.DMA((2,))],
        compiler_params=pltpu.CompilerParams(vmem_limit_bytes=48 * 1024 * 1024),
        name="transport",
    )(decay, obs_weight, release_cells[0], adjoint_end, rim, water_mask, mixing, *arrivals)
    gathered = lax.all_to_all(samples, ("rcpt", "space"), split_axis=0, concat_axis=0, tiled=True)
    strips = lax.axis_size("space")
    gathered = gathered.reshape(batches, strips, channels + recv, cells)
    group = 4
    own_blocks, depth, scenarios = profiles.shape[1:]
    result = pl.pallas_call(
        response_kernel,
        grid=(strips // group,),
        out_shape=jax.ShapeDtypeStruct((strips, own_blocks, batches * recv, scenarios), f32),
        in_specs=[
            pl.BlockSpec((batches, group, channels + recv, cells), lambda s: (0, s, 0, 0)),
            pl.BlockSpec((group, own_blocks, depth, scenarios), lambda s: (s, 0, 0, 0)),
        ],
        out_specs=pl.BlockSpec((group, own_blocks, batches * recv, scenarios), lambda s: (s, 0, 0, 0)),
        compiler_params=pltpu.CompilerParams(vmem_limit_bytes=16_000_000),
        name="response",
    )(gathered, profiles)
    return (start, result)


def solution(mesh):
    placed = (
        P("rcpt", None, "space", None),
        P("rcpt", None, None, "space", None),
        P(),
        P("space", None),
        P(None, "space", None),
        P("rcpt"),
        P(None, "rcpt"),
        P("space", None, None),
        P(None, ("rcpt", "space"), None, None),
    )
    return jax.shard_map(
        on_device,
        mesh=mesh,
        in_specs=placed,
        out_specs=(P("rcpt", None, "space", None), P(None, ("rcpt", "space"), None, None)),
        check_vma=False,
    )
```

```python
import functools

import jax
import jax.numpy as jnp
from jax import lax
from jax.experimental import pallas as pl
from jax.experimental.pallas import tpu as pltpu
from jax.sharding import PartitionSpec as P


HOURS = 4
RIM = 4
LANES = 128


diffusion_number = 0.08


SCALE_STEPS = 64
LARGEST = 32700.0


def encode(samples, recv):
    channels, cells = samples.shape
    levels = channels // recv
    reach = jnp.maximum(jnp.max(jnp.abs(samples), axis=1, keepdims=True), 1e-30)
    power = jnp.ceil(jnp.log2(reach) * SCALE_STEPS)
    codes = jnp.round(samples * (LARGEST * jnp.exp2(power * (-1.0 / SCALE_STEPS))))
    part = lax.broadcasted_iota(jnp.int32, (recv, cells), 1) // (cells // levels)
    powers = jnp.broadcast_to(power[:recv], (recv, cells))
    for l in range(1, levels):
        powers = jnp.where(part == l, power[l * recv:(l + 1) * recv], powers)
    return jnp.concatenate([codes, powers], axis=0).astype(jnp.int32).astype(jnp.int16)


def prepare_kernel(
    adj_hbm, rim_hbm, water_hbm, mix_hbm, origin, masks, mix, water_in, water, sem_in, sem_origin
):
    levels, slots, recv, _ = origin.shape
    tiles = water.shape[0]
    own = slots - 2 * RIM
    copies = [pltpu.make_async_copy(water_hbm, water_in, sem_in)]
    for j in range(tiles):
        lanes = pl.ds(j * LANES, LANES)
        copies.append(pltpu.make_async_copy(mix_hbm.at[:, :, lanes], mix.at[:, j, pl.ds(0, own)], sem_in))
        copies.append(
            pltpu.make_async_copy(
                rim_hbm.at[pl.ds(levels * recv + 1, levels - 1), :, lanes],
                mix.at[:, j, pl.ds(own, 2 * RIM)],
                sem_in,
            )
        )
        copies.append(
            pltpu.make_async_copy(
                rim_hbm.at[levels * recv, :, lanes], water.at[j, pl.ds(8 + own, 2 * RIM)], sem_in
            )
        )
    origin_copies = []
    for r in range(recv):
        origin_copies.append(
            pltpu.make_async_copy(adj_hbm.at[r], origin.at[:, pl.ds(0, own), r, :], sem_origin)
        )
        origin_copies.append(
            pltpu.make_async_copy(
                rim_hbm.at[pl.ds(r * levels, levels)],
                origin.at[:, pl.ds(own, 2 * RIM), r, :],
                sem_origin,
            )
        )
    for copy in copies + origin_copies:
        copy.start()
    for copy in copies:
        copy.wait()

    lane = lax.broadcasted_iota(jnp.int32, (8, LANES), 1)
    first = lane == 0
    last = lane == LANES - 1

    for j in range(tiles):
        lanes = slice(j * LANES, (j + 1) * LANES)
        for g in range(own // 8):
            water[j, 8 + g * 8:16 + g * 8, :] = water_in[g * 8:g * 8 + 8, lanes].astype(jnp.float32)
        water[j, 7:8, :] = water[j, 7 + slots:8 + slots, :]
        water[j, 8 + slots:9 + slots, :] = water[j, 8:9, :]

    def mask_rows(g, carry):
        base = pl.multiple_of(8 + g * 8, 8)
        here = [water[j, pl.ds(base, 8), :] for j in range(tiles)]
        right = [pltpu.roll(v, LANES - 1, 1) for v in here]
        left = [pltpu.roll(v, 1, 1) for v in here]
        rows = pl.ds(pl.multiple_of(g * 8, 8), 8)
        for j in range(tiles):
            masks[0, j, rows, :] = here[j]
            masks[1, j, rows, :] = here[j] * water[j, pl.ds(base + 1, 8), :]
            masks[2, j, rows, :] = here[j] * water[j, pl.ds(base - 1, 8), :]
            beyond = right[j + 1] if j + 1 < tiles else jnp.zeros_like(lane, jnp.float32)
            before = left[j - 1] if j > 0 else jnp.zeros_like(lane, jnp.float32)
            masks[3, j, rows, :] = here[j] * jnp.where(last, beyond, right[j])
            masks[4, j, rows, :] = here[j] * jnp.where(first, before, left[j])
        return carry

    lax.fori_loop(0, slots // 8, mask_rows, 0)
    for copy in origin_copies:
        copy.wait()


def transport_kernel(
    decay_ref, obs_ref, origin, masks, mix, cells_hbm,
    p0, p1, p2, p3, q0, q1, q2, q3,
    start_hbm, samples_hbm,
    field_a, field_b, cur, weights, table, picked, outgoing,
    cell_slots, sem_cur, sem_out, sem_samples, sem_cells,
):
    levels, slots, recv, _ = origin.shape
    tiles = masks.shape[1]
    own = slots - 2 * RIM
    x_here = lax.axis_index("rcpt") // 2
    depth = p0.shape[1]
    cur_copies = []
    for dx, (piece, piece_rim) in enumerate(((p0, q0), (p1, q1), (p2, q2), (p3, q3))):
        to = pl.ds(lax.rem(x_here + dx, 4) * depth, depth)
        cur_copies.append(pltpu.make_async_copy(piece, cur.at[:, to, pl.ds(0, own)], sem_cur))
        cur_copies.append(
            pltpu.make_async_copy(piece_rim, cur.at[pl.ds(1, HOURS - 1), to, pl.ds(own, 2 * RIM)], sem_cur)
        )

    for copy in cur_copies:
        copy.start()

    cell_ring, held, _ = cell_slots.shape

    def cells_copy(i, slot):
        return pltpu.make_async_copy(
            cells_hbm.at[pl.ds(i * held, held)], cell_slots.at[slot], sem_cells.at[slot]
        )

    for slot in range(cell_ring):
        cells_copy(slot, slot).start()

    lane = lax.broadcasted_iota(jnp.int32, (8, LANES), 1)
    first = lane == 0
    last = lane == LANES - 1

    for copy in cur_copies:
        copy.wait()

    sublane = lax.broadcasted_iota(jnp.int32, (recv, LANES), 0)

    def per_receptor(read):
        spread = jnp.zeros((recv, LANES), jnp.float32)
        for r in range(recv):
            spread = jnp.where(sublane == r, read(r), spread)
        return spread

    keep = per_receptor(lambda r: 1.0 - decay_ref[r])
    for step in range(HOURS):
        hour = HOURS - 1 - step

        def weigh(i, carry):
            g = lax.rem(i, slots // 8)
            l = i // (slots // 8)
            rows = pl.ds(pl.multiple_of(g * 8, 8), 8)
            for j in range(tiles):
                lanes = slice(j * LANES, (j + 1) * LANES)
                u = cur[hour, l, rows, lanes].astype(jnp.float32)
                v = cur[hour, levels + l, rows, lanes].astype(jnp.float32)
                down = (jnp.maximum(u, 0.0) + diffusion_number) * masks[1, j, rows, :]
                up = (jnp.maximum(-u, 0.0) + diffusion_number) * masks[2, j, rows, :]
                right = (jnp.maximum(v, 0.0) + diffusion_number) * masks[3, j, rows, :]
                left = (jnp.maximum(-v, 0.0) + diffusion_number) * masks[4, j, rows, :]
                weights[0, l, j, rows, :] = masks[0, j, rows, :] - ((down + up) + (right + left))
                weights[1, l, j, rows, :] = down
                weights[2, l, j, rows, :] = up
                weights[3, l, j, rows, :] = right
                weights[4, l, j, rows, :] = left
            return carry

        lax.fori_loop(0, levels * (slots // 8), weigh, 0, unroll=4)

        reach = HOURS - 1 - step
        old = (origin, field_a, field_b, field_a)[step]
        new = (field_a, field_b, field_a, field_b)[step]
        kept = keep if step == 0 else kept * keep
        obs = per_receptor(lambda r: obs_ref[hour, r]) / kept
        is_last = step == HOURS - 1

        def advance(i, carry):
            row = i - reach
            at = jnp.where(row < 0, row + slots, row)
            below = jnp.where(at == slots - 1, 0, at + 1)
            above = jnp.where(at == 0, slots - 1, at - 1)
            here = pl.ds(at, 1)
            value = [[None] * levels for _ in range(tiles)]
            turn_r = [[None] * levels for _ in range(tiles)]
            turn_l = [[None] * levels for _ in range(tiles)]

            def fetch(j):
                lanes = slice(j * LANES, (j + 1) * LANES)
                for l in range(levels):
                    v = old[l, at, :, lanes]
                    value[j][l] = v
                    turn_r[j][l] = pltpu.roll(v, LANES - 1, 1)
                    turn_l[j][l] = pltpu.roll(v, 1, 1)

            fetch(0)
            for j in range(tiles):
                lanes = slice(j * LANES, (j + 1) * LANES)
                if j + 1 < tiles:
                    fetch(j + 1)
                forced = obs * masks[0, j, here, :]
                moved = []
                for l in range(levels):
                    beyond = turn_r[j + 1][l] if j + 1 < tiles else turn_r[j][l]
                    before = turn_l[j - 1][l] if j > 0 else turn_l[j][l]
                    east = jnp.where(last, beyond, turn_r[j][l])
                    west = jnp.where(first, before, turn_l[j][l])
                    acc = weights[0, l, j, here, :] * value[j][l]
                    acc = acc + weights[1, l, j, here, :] * old[l, below, :, lanes]
                    acc = acc + weights[2, l, j, here, :] * old[l, above, :, lanes]
                    acc = acc + weights[3, l, j, here, :] * east
                    acc = acc + weights[4, l, j, here, :] * west
                    moved.append(acc)
                flux = [mix[k, j, here, :] * (moved[k + 1] - moved[k]) for k in range(levels - 1)]
                results = []
                for l in range(levels):
                    mixed = moved[l]
                    if l < levels - 1:
                        mixed = mixed + flux[l]
                    if l > 0:
                        mixed = mixed - flux[l - 1]
                    result = mixed + forced * origin[l, at, :, lanes]
                    if is_last:
                        result = kept * result
                    results.append(result)
                    new[l, at, :, lanes] = result
            return carry

        lax.fori_loop(0, own + 2 * reach, advance, 0, unroll=4 if (own + 2 * reach) % 4 == 0 else 2)

    out_copies = [
        pltpu.make_async_copy(field_b.at[:, pl.ds(0, own), r, :], start_hbm.at[r], sem_out)
        for r in range(recv)
    ]
    for copy in out_copies:
        copy.start()

    def tabulate(row, carry):
        for j in range(tiles):
            lanes = slice(j * LANES, (j + 1) * LANES)
            stack = jnp.concatenate([field_b[l, row, :, lanes] for l in range(levels)], axis=0)
            at = pl.multiple_of((row * tiles + j) * LANES, LANES)
            table[pl.ds(at, LANES), :] = stack.T
        return carry

    lax.fori_loop(0, own, tabulate, 0, unroll=4)

    channels = levels * recv
    blocks = cells_hbm.shape[0]
    rounds = blocks // held // cell_ring

    def samples_copy(i, slot):
        at = pl.ds((i * cell_ring + slot) * held, held)
        return pltpu.make_async_copy(outgoing.at[at], samples_hbm.at[at], sem_samples)

    def pick(i, carry):
        for slot in range(cell_ring):
            cells_copy(i * cell_ring + slot, slot).wait()
            for k in range(held):
                for c in range(LANES):
                    picked[k % 4, c:c + 1, :] = table[pl.ds(cell_slots[slot, k, c], 1), :]
                outgoing[(i * cell_ring + slot) * held + k] = encode(picked[k % 4].T, recv)
            samples_copy(i, slot).start()
            cells_copy(jnp.minimum(i + 1, rounds - 1) * cell_ring + slot, slot).start()
        return carry

    lax.fori_loop(0, rounds, pick, 0)
    for slot in range(cell_ring):
        cells_copy(slot, slot).wait()
    for copy in out_copies:
        copy.wait()
    pltpu.make_async_copy(outgoing, samples_hbm, sem_samples).wait()


def response_kernel(samples_ref, profiles_ref, out_ref):
    batches, strips, rows, cells = samples_ref.shape
    levels = profiles_ref.shape[2] // cells
    recv = rows // (levels + 1)
    for s in range(strips):
        coded = samples_ref[:, s].astype(jnp.int32).astype(jnp.float32)
        scales = jnp.exp2(coded[:, levels * recv:] * (1.0 / SCALE_STEPS)) * (1.0 / LARGEST)
        parts = []
        for l in range(levels):
            lane = l * (cells // levels)
            left = coded[:, l * recv:(l + 1) * recv] * scales[:, :, lane:lane + 1]
            parts.append(left.reshape(batches * recv, cells))
        left = jnp.concatenate(parts, axis=1)
        left_hi = left.astype(jnp.bfloat16)
        left_lo = (left - left_hi.astype(jnp.float32)).astype(jnp.bfloat16)
        right = profiles_ref[s, 0]
        right_hi = right.astype(jnp.bfloat16)
        right_lo = (right - right_hi.astype(jnp.float32)).astype(jnp.bfloat16)
        both = jnp.concatenate([left_hi, left_lo], axis=0)
        first = jnp.dot(both, right_hi, preferred_element_type=jnp.float32)
        second = jnp.dot(left_hi, right_lo, preferred_element_type=jnp.float32)
        half = batches * recv
        out_ref[s, 0] = first[:half] + (first[half:] + second)


def shift_rims(upper, lower, dim):
    count = lax.axis_size("space")
    forward = [(i, i + 1) for i in range(count - 1)]
    backward = [(b, a) for a, b in forward]
    low = lax.ppermute(upper, "space", forward)
    high = lax.ppermute(lower, "space", backward)
    return jnp.concatenate([high, low], axis=dim)


def on_device(
    adjoint_end, currents, plan, water_mask, mixing, decay, obs_weight, release_cells, profiles
):
    recv, levels, own, width = adjoint_end.shape
    batches = lax.axis_size("rcpt")
    x_count = batches // 2
    slots = own + 2 * RIM

    pieces = currents.reshape(x_count, -1, own, width)
    depth = pieces.shape[1]
    pieces = jnp.concatenate([pieces, pieces], axis=1).reshape(batches, depth, own, width)
    with jax.named_scope("spread"):
        pieces = lax.all_to_all(pieces, "rcpt", split_axis=0, concat_axis=0, tiled=True)
    wanted = jnp.take(pieces, plan, axis=0, mode="clip")
    routes = [[(i, (i - 2 * dx) % batches) for i in range(batches)] for dx in range(1, x_count)]
    with jax.named_scope("gather"):
        arrivals = [wanted] + [lax.ppermute(wanted, "rcpt", route) for route in routes]
    with jax.named_scope("cur_rim"):
        cur_rim = shift_rims(wanted[1:, :, own - RIM:], wanted[1:, :, :RIM], 2)
        arrivals += [cur_rim] + [lax.ppermute(cur_rim, "rcpt", route) for route in routes]

    edges = jnp.concatenate(
        [
            adjoint_end.reshape(recv * levels, own, width),
            water_mask.astype(jnp.float32)[None],
            mixing,
        ],
        axis=0,
    )
    with jax.named_scope("field_rim"):
        rim = shift_rims(edges[:, own - RIM:], edges[:, :RIM], 1)

    tiles = width // LANES
    blocks, cells = release_cells.shape[1:]
    channels = recv * levels
    hbm = pl.BlockSpec(memory_space=pl.ANY)
    smem = pl.BlockSpec(memory_space=pltpu.SMEM)
    f32 = jnp.float32
    vmem = pl.BlockSpec(memory_space=pltpu.VMEM)
    field_shape = (levels, slots, recv, width)
    origin, masks, mix = pl.pallas_call(
        prepare_kernel,
        out_shape=(
            jax.ShapeDtypeStruct(field_shape, f32),
            jax.ShapeDtypeStruct((5, tiles, slots, LANES), f32),
            jax.ShapeDtypeStruct((levels - 1, tiles, slots, LANES), f32),
        ),
        in_specs=[hbm] * 4,
        out_specs=(vmem, vmem, vmem),
        scratch_shapes=[
            pltpu.VMEM((own, width), jnp.int32),
            pltpu.VMEM((tiles, slots + 16, LANES), f32),
        ]
        + [pltpu.SemaphoreType.DMA] * 2,
        compiler_params=pltpu.CompilerParams(vmem_limit_bytes=16 * 1024 * 1024),
        cost_estimate=pl.CostEstimate(flops=0, bytes_accessed=16_000_000, transcendentals=0),
        name="prepare",
    )(adjoint_end, rim, water_mask, mixing)
    start, samples = pl.pallas_call(
        transport_kernel,
        out_shape=(
            jax.ShapeDtypeStruct((recv, levels, own, width), f32),
            jax.ShapeDtypeStruct((blocks, channels + recv, cells), jnp.int16),
        ),
        in_specs=[smem, smem, vmem, vmem, vmem] + [hbm] * 9,
        out_specs=(hbm, hbm),
        scratch_shapes=[
            pltpu.VMEM(field_shape, f32),
            pltpu.VMEM(field_shape, f32),
            pltpu.VMEM((HOURS, 2 * levels, slots, width), jnp.bfloat16),
            pltpu.VMEM((5, levels, tiles, slots, LANES), f32),
            pltpu.VMEM((own * width, channels), f32),
            pltpu.VMEM((4, cells, channels), f32),
            pltpu.VMEM((blocks, channels + recv, cells), jnp.int16),
            pltpu.SMEM((2, 16, cells), jnp.int32),
        ]
        + [pltpu.SemaphoreType.DMA] * 3
        + [pltpu.SemaphoreType.DMA((2,))],
        compiler_params=pltpu.CompilerParams(vmem_limit_bytes=42 * 1024 * 1024),
        name="transport",
    )(decay, obs_weight, origin, masks, mix, release_cells[0], *arrivals)
    gathered = lax.all_to_all(samples, ("rcpt", "space"), split_axis=0, concat_axis=0, tiled=True)
    strips = lax.axis_size("space")
    gathered = gathered.reshape(batches, strips, channels + recv, cells)
    group = 4
    own_blocks, depth, scenarios = profiles.shape[1:]
    result = pl.pallas_call(
        response_kernel,
        grid=(strips // group,),
        out_shape=jax.ShapeDtypeStruct((strips, own_blocks, batches * recv, scenarios), f32),
        in_specs=[
            pl.BlockSpec((batches, group, channels + recv, cells), lambda s: (0, s, 0, 0)),
            pl.BlockSpec((group, own_blocks, depth, scenarios), lambda s: (s, 0, 0, 0)),
        ],
        out_specs=pl.BlockSpec((group, own_blocks, batches * recv, scenarios), lambda s: (s, 0, 0, 0)),
        compiler_params=pltpu.CompilerParams(vmem_limit_bytes=16_000_000),
        name="response",
    )(gathered, profiles)
    return (start, result)


def solution(mesh):
    placed = (
        P("rcpt", None, "space", None),
        P("rcpt", None, None, "space", None),
        P(),
        P("space", None),
        P(None, "space", None),
        P("rcpt"),
        P(None, "rcpt"),
        P("space", None, None),
        P(None, ("rcpt", "space"), None, None),
    )
    return jax.shard_map(
        on_device,
        mesh=mesh,
        in_specs=placed,
        out_specs=(P("rcpt", None, "space", None), P(None, ("rcpt", "space"), None, None)),
        check_vma=False,
    )
```
